256 devices in a mesh: samp: 4 (over x), snp: 4 (over z_lo, core), gene: 16 (over z_hi, y).
Axes of the slice: x: 4, y: 4, z: 8 (z_hi: 4, z_lo: 2; z = z_hi * 2 + z_lo), core: 2. Of those that a mesh axis runs over, the one named last changes fastest.
Arguments:
- dosage: bfloat16 [18432, 1024], P(('samp', 'gene'), 'snp'), may hold values from 0 to 2
- snp_scale: float32 [1024], P('snp'), may hold values from 0.5 to 2
- covariates: float32 [18432, 64], P(('samp', 'gene'))
- previous: bfloat16 [18432, 1024], P(('samp', 'gene'), 'snp')
- expression: bfloat16 [18432, 20480], P('samp', 'gene')
Outputs:
- resid: bfloat16 [18432, 1024], P(('samp', 'gene'), 'snp')
- zscores: bfloat16 [1024, 20480], P('snp', 'gene')
The draws below stay inside these ranges and needn't reach their ends.
All inputs are finite; a program needn't handle non-finite values.
Results may differ from the reference program's by a relative error of at most 0.001.
Values may be sent and summed in bfloat16 or wider, within the bound.
A program may use at most 128 MiB of HBM per device.

```python
import math
import jax
import jax.numpy as jnp
from jax import lax

SNPS = 1024
GENES = 20480
COVS = 64
SAMPLES = 18432
N_GENE = 16


def sample_rise(count, top):
    position = jnp.arange(count).astype(jnp.float32)
    return 10.0 ** (top * position / count)


def shared_parts(key):
    base = jax.random.fold_in(key, 101)
    first, second, third = jax.random.split(base, 3)
    drawn = jax.random.normal(first, (SAMPLES, COVS), jnp.float32)
    mixing = jax.random.normal(second, (COVS, SNPS), jnp.float32)
    noise = jax.random.normal(third, (SAMPLES, SNPS), jnp.float32)
    return (drawn, mixing, noise)


def draw_covariates(key, part):
    drawn, mixing, noise = shared_parts(key)
    top = 0.5
    return drawn * sample_rise(SAMPLES, top)[:, None]


def draw_dosage(key, part):
    drawn, mixing, noise = shared_parts(key)
    latent = jnp.dot(drawn, mixing) / jnp.sqrt(jnp.float32(COVS))
    return (1.0 + 0.9 * jnp.tanh(0.8 * latent + 0.6 * noise)).astype(jnp.bfloat16)


def draw_previous(key, part):
    base = jax.random.fold_in(key, 202)
    first, second = jax.random.split(base, 2)
    top = 0.25
    values = jax.random.normal(first, (SAMPLES, SNPS), jnp.float32)
    column = 10.0 ** jax.random.uniform(second, (SNPS,), jnp.float32)
    return (values * sample_rise(SAMPLES, top)[:, None] * column[None, :]).astype(jnp.bfloat16)


def draw_expression(key, part):
    base = jax.random.fold_in(key, 303)
    first, second = jax.random.split(base, 2)
    values = jax.random.normal(first, (SAMPLES, GENES), jnp.float32)
    column = 10.0 ** jax.random.uniform(second, (GENES,), jnp.float32)
    top = 0.25
    return (values * sample_rise(SAMPLES, top)[:, None] * column[None, :]).astype(jnp.bfloat16)


def shard_levels(rng, shape, cuts, smallest, largest):
    level, own = 1.0, jax.random.fold_in(rng, 6)
    for axis_at, parts in cuts:
        heights = jnp.exp(jax.random.uniform(jax.random.fold_in(own, axis_at), (parts,), jnp.float32, smallest / len(cuts), largest / len(cuts)))
        level = level * jnp.repeat(heights, shape[axis_at] // parts).reshape([-1 if axis == axis_at else 1 for axis in range(len(shape))])
    return level


def setup_inputs(seed: int = 0) -> dict:
    key_list = jax.random.split(jax.random.key(seed), 6)
    dosage = draw_dosage(jax.random.fold_in(key_list[5], 71), 0)
    snp_scale = jnp.clip(jnp.exp(math.log(2.0) - 1.3862944 * jax.random.uniform(key_list[1], (SNPS,), jnp.float32) ** shard_levels(key_list[1], (SNPS,), ((0, 4),), -0.2, 0.2)), 0.5, 2.0)
    covariates = draw_covariates(jax.random.fold_in(key_list[5], 71), 0)
    previous = draw_previous(jax.random.fold_in(key_list[5], 71), 0)
    expression = draw_expression(jax.random.fold_in(key_list[5], 71), 0)
    return {"dosage": dosage, "snp_scale": snp_scale, "covariates": covariates, "previous": previous, "expression": expression}


def reference(dosage, snp_scale, covariates, previous, expression):
    highest = lax.Precision.HIGHEST
    decoded = dosage.astype(jnp.float32) * snp_scale[None, :]
    gram = jnp.dot(covariates.T, covariates, precision=highest)
    cross = jnp.dot(covariates.T, decoded, precision=highest)
    factor = jnp.linalg.cholesky(gram)
    coef = jax.scipy.linalg.cho_solve((factor, True), cross)
    resid = (decoded - jnp.dot(covariates, coef, precision=highest)).astype(jnp.bfloat16)
    genotype = previous.astype(jnp.float32)
    panels = expression.reshape(SAMPLES, N_GENE, GENES // N_GENE).transpose(1, 0, 2)

    def panel_scores(panel):
        return jnp.dot(genotype.T, panel.astype(jnp.float32), precision=highest)
    scores = lax.map(panel_scores, panels).transpose(1, 0, 2).reshape(SNPS, GENES)
    x_sq = lax.optimization_barrier(jnp.sum(genotype * genotype, axis=0))
    y_sq = jnp.einsum('sg,sg->g', expression.astype(jnp.float32), expression.astype(jnp.float32), preferred_element_type=jnp.float32)
    denom = jnp.sqrt(x_sq + 1e-06)[:, None] * jnp.sqrt(y_sq + 1e-06)[None, :]
    zscores = (jnp.sqrt(jnp.float32(SAMPLES)) * scores / denom).astype(jnp.bfloat16)
    return (resid, zscores)
```

```python
import jax
import jax.numpy as jnp
from jax import lax
from jax.experimental import pallas as pl
from jax.experimental.pallas import tpu as pltpu
from jax.sharding import PartitionSpec as P

F32 = jnp.float32
BF16 = jnp.bfloat16
HIGHEST = lax.Precision.HIGHEST
N = 4
ROWS = 288
CUT = 144
PANEL = N * ROWS
SNP = 256
HALF = 128
GENES = 1280
WIDE = GENES + 128
SPLIT = 768
OWN = HALF // N
COVS = 64
AUG = 384
SHARE = COVS // N
SAMPLES = 18432


def kernel(
    dosage_hbm, scale_ref, cov_hbm, prev_hbm, expr_hbm,
    resid_hbm, z_hbm,
    expr, geno, dose, cov, part, from_x, from_y, from_z, sums, full, system,
    ysq, from_ysq, acc, hop1, hop2, stat, resid,
    load_sem, send, recv, store_sem,
):
    s = lax.axis_index("samp")
    gene = lax.axis_index("gene")
    zh, y = gene // N, gene % N

    def peer(axis, step):
        if axis == "x":
            return {"samp": (s + step + N) % N}
        if axis == "y":
            return {"gene": zh * N + (y + step + N) % N}
        return {"gene": ((zh + step + N) % N) * N + y}

    loads = [
        pltpu.make_async_copy(cov_hbm, cov, load_sem.at[0]),
        pltpu.make_async_copy(dosage_hbm, dose, load_sem.at[1]),
        pltpu.make_async_copy(prev_hbm.at[:, pl.ds(0, HALF)], geno.at[0, 0, pl.ds(0, ROWS)], load_sem.at[2]),
        pltpu.make_async_copy(prev_hbm.at[:, pl.ds(HALF, HALF)], geno.at[1, 0, pl.ds(0, ROWS)], load_sem.at[3]),
    ]
    for c in loads:
        c.start()
    panels = {}
    for ry in (0, 3, 1, 2):
        for rz in range(N):
            block = ((zh + rz) % N) * N + (y + ry) % N
            c = pltpu.make_async_copy(
                expr_hbm.at[pl.ds(pl.multiple_of(block * ROWS, 16), ROWS)],
                expr.at[ry, pl.ds(rz * ROWS, ROWS)],
                load_sem.at[4 + ry * N + rz],
            )
            c.start()
            panels[ry, rz] = c

    peers = [peer(a, d) for a in "xyz" for d in (1, 2, 3)]
    barrier = pltpu.get_barrier_semaphore()
    for device in peers:
        pl.semaphore_signal(barrier, inc=1, device_id=device, device_id_type=pl.DeviceIdType.MESH)

    loads[0].wait()
    loads[1].wait()
    cov_t = cov[...].T
    part[:, :SNP] = jnp.dot(cov_t, dose[...].astype(F32), precision=HIGHEST, preferred_element_type=F32)
    part[:, SNP:] = jnp.zeros((COVS, AUG - SNP), F32)
    part[:, SNP : SNP + COVS] = jnp.dot(cov_t, cov[...], precision=HIGHEST, preferred_element_type=F32)
    loads[2].wait()
    loads[3].wait()
    pl.semaphore_wait(barrier, len(peers))

    sent = []
    ids = {}

    def push(name, src, dst, axis, step):
        t = len(sent)
        c = pltpu.make_async_remote_copy(
            src_ref=src, dst_ref=dst, send_sem=send.at[t], recv_sem=recv.at[t],
            device_id=peer(axis, step), device_id_type=pl.DeviceIdType.MESH,
        )
        c.start()
        sent.append(c)
        ids[name] = c

    def arrive(*names):
        for name in names:
            ids[name].wait_recv()

    def rows(rz, lo=0, n=ROWS):
        return pl.ds(rz * ROWS + lo, n)

    def z_own(h):
        for step in (1, -1):
            to = -step % N
            push(("z", h, to), geno.at[h, 0, rows(0)], geno.at[h, 0, rows(to)], "z", step)

    def z_pass(h):
        arrive(("z", h, 3))
        push(("z", h, 2, 0), geno.at[h, 0, rows(3, 0, CUT)], geno.at[h, 0, rows(2, 0, CUT)], "z", 1)
        arrive(("z", h, 1))
        push(("z", h, 2, 1), geno.at[h, 0, rows(1, CUT, CUT)], geno.at[h, 0, rows(2, CUT, CUT)], "z", -1)

    def z_last(h):
        arrive(("z", h, 2, 0), ("z", h, 2, 1))

    def y_own(h, rz):
        for step in (1, -1):
            to = -step % N
            push(("y", h, to, rz), geno.at[h, 0, rows(rz)], geno.at[h, to, rows(rz)], "y", step)

    def y_pass(h, rz):
        arrive(("y", h, 3, rz))
        push(("y", h, 2, rz, 0), geno.at[h, 3, rows(rz, 0, CUT)], geno.at[h, 2, rows(rz, 0, CUT)], "y", 1)
        arrive(("y", h, 1, rz))
        push(("y", h, 2, rz, 1), geno.at[h, 1, rows(rz, CUT, CUT)], geno.at[h, 2, rows(rz, CUT, CUT)], "y", -1)

    def y_last(h):
        for rz in (0, 3, 1, 2):
            arrive(("y", h, 2, rz, 0), ("y", h, 2, rz, 1))

    def share(q):
        return pl.ds(pl.multiple_of(((s + q) % N) * SHARE, SHARE), SHARE)

    def cov_out():
        for q in (1, 3, 2):
            push(("cx", q), part.at[share(q)], from_x.at[q - 1], "x", q)

    def cov_step(axis_in, landed, base, slot, axis_out, landing, tag):
        arrive(*[(axis_in, q) for q in (1, 3, 2)])
        sums[slot] = base + landed[0] + landed[1] + landed[2]
        for q in (1, 3, 2):
            if landing is None:
                push((tag, q), sums.at[slot], full.at[N - q], axis_out, q)
            else:
                push((tag, q), sums.at[slot], landing.at[q - 1], axis_out, q)

    def square_block(ry, rz):
        panels[ry, rz].wait()

        def body(i, total):
            e = expr[ry, pl.ds(pl.multiple_of(rz * ROWS + i * 16, 16), 16), :].astype(F32)
            e = e * e
            return total + e[:8] + e[8:]

        ysq[...] += lax.fori_loop(0, ROWS // 16, body, jnp.zeros((8, GENES), F32), unroll=2)

    def ysq_out():
        for q in (1, 3, 2):
            push(("q", q), ysq, from_ysq.at[q - 1], "x", q)

    def scores(h, ry, first):
        lhs = geno[h, ry].T
        f = lhs.astype(F32)
        f = f * f
        squares = f[:, :128]
        for i in range(1, PANEL // 128):
            squares = squares + f[:, i * 128 : (i + 1) * 128]
        acc[h, :, GENES:] = squares if first else acc[h, :, GENES:] + squares

        @pl.loop(0, GENES // 256)
        def _(j):
            at = pl.ds(pl.multiple_of(j * 256, 256), 256)
            d = jnp.dot(lhs, expr[ry, :, at], preferred_element_type=F32)
            acc[h, :, at] = d if first else acc[h, :, at] + d

    def piece(q):
        return pl.ds(pl.multiple_of(((s + q + N) % N) * OWN, OWN), OWN)

    lo, hi = pl.ds(0, SPLIT), pl.ds(SPLIT, WIDE - SPLIT)

    def reduce_out(h):
        push(("r", h, 0), acc.at[h, piece(2), lo], hop1.at[h, :, lo], "x", 1)
        push(("r", h, 1), acc.at[h, piece(2), hi], hop1.at[h, :, hi], "x", -1)

    def reduce_pass(h):
        arrive(("r", h, 0))
        acc[h, piece(1), lo] += hop1[h, :, lo]
        push(("r2", h, 0), acc.at[h, piece(1)], hop2.at[h, 0], "x", 1)
        arrive(("r", h, 1))
        acc[h, piece(-1), hi] += hop1[h, :, hi]
        push(("r2", h, 1), acc.at[h, piece(-1)], hop2.at[h, 1], "x", -1)

    def normalise(h):
        y_total = ysq[...] + from_ysq[0] + from_ysq[1] + from_ysq[2]
        y_factor = 1.0 / jnp.sqrt(jnp.sum(y_total, axis=0, keepdims=True) + 1e-6)
        arrive(("r2", h, 0), ("r2", h, 1))
        total = acc[h, piece(0)] + hop2[h, 0] + hop2[h, 1]
        x_total = jnp.sum(total[:, GENES:], axis=1, keepdims=True)
        x_factor = jnp.sqrt(F32(SAMPLES)) / jnp.sqrt(x_total + 1e-6)
        stat[h, 0] = (total[:, :GENES] * x_factor * y_factor).astype(BF16)
        for step in (1, -1):
            push(("s", h, -step % N), stat.at[h, 0], stat.at[h, -step % N], "x", step)

    def stat_pass(h):
        half = OWN // 2
        arrive(("s", h, 3))
        push(("s", h, 2, 0), stat.at[h, 3, pl.ds(0, half)], stat.at[h, 2, pl.ds(0, half)], "x", 1)
        arrive(("s", h, 1))
        push(("s", h, 2, 1), stat.at[h, 1, pl.ds(half, half)], stat.at[h, 2, pl.ds(half, half)], "x", -1)

    stores = []

    def stat_store(h, q):
        start = pl.multiple_of(h * HALF + ((s + q) % N) * OWN, OWN)
        c = pltpu.make_async_copy(stat.at[h, q], z_hbm.at[pl.ds(start, OWN)], store_sem.at[h * N + q])
        c.start()
        stores.append(c)

    def stat_done(h):
        for q in (0, 3, 1):
            stat_store(h, q)
        arrive(("s", h, 2, 0), ("s", h, 2, 1))
        stat_store(h, 2)

    lane = lax.broadcasted_iota(jnp.int32, (COVS, 128), 1)
    line = lax.broadcasted_iota(jnp.int32, (COVS, AUG), 0)

    def gather_system():
        arrive(*[("cf", q) for q in (1, 3, 2)])
        system[share(0)] = sums[2]
        for q in (1, 2, 3):
            system[share(q)] = full[q]

    def eliminate(start, count):
        def body(k, carry):
            a = system[...]
            row = system[pl.ds(k, 1), :]
            col = jnp.sum(jnp.where(lane == k, a[:, SNP:], 0.0), axis=1, keepdims=True)
            pivot = jnp.sum(jnp.where(lane[:1] == k, row[:, SNP:], 0.0), axis=1, keepdims=True)
            row = row / pivot
            system[...] = jnp.where(line == k, row, a - col * row)
            return carry

        lax.fori_loop(start, start + count, body, 0)

    def residual():
        fit = jnp.dot(cov[...], system[:, :SNP], precision=HIGHEST, preferred_element_type=F32)
        resid[...] = ((dose[...].astype(F32) - fit) * scale_ref[...]).astype(BF16)
        c = pltpu.make_async_copy(resid, resid_hbm, store_sem.at[2 * N])
        c.start()
        stores.append(c)

    ysq[...] = jnp.zeros((8, GENES), F32)
    z_own(0)
    y_own(0, 0)
    cov_out()
    for rz in range(N):
        square_block(0, rz)
    y_pass(0, 0)
    cov_step("cx", from_x, part[share(0)], 0, "y", from_y, "cy")
    for rz in range(2):
        square_block(3, rz)
    z_pass(0)
    y_own(0, 3)
    y_own(0, 1)
    z_own(1)
    for rz in range(2, 4):
        square_block(3, rz)
    cov_step("cy", from_y, sums[0], 1, "z", from_z, "cz")
    z_last(0)
    y_own(0, 2)
    y_own(1, 0)
    y_pass(0, 3)
    for rz in range(4):
        square_block(1, rz)
    y_pass(0, 1)
    cov_step("cz", from_z, sums[1], 2, "x", None, "cf")
    z_pass(1)
    for rz in range(4):
        square_block(2, rz)
    ysq_out()
    y_own(1, 3)
    y_own(1, 1)
    y_pass(0, 2)
    scores(0, 0, True)
    z_last(1)
    y_own(1, 2)
    scores(0, 3, False)
    scores(0, 1, False)
    y_pass(1, 0)
    y_last(0)
    scores(0, 2, False)
    reduce_out(0)
    gather_system()
    eliminate(0, 16)
    y_pass(1, 3)
    eliminate(16, 8)
    reduce_pass(0)
    y_pass(1, 1)
    eliminate(24, 16)
    y_pass(1, 2)
    scores(1, 0, True)
    arrive(*[("q", q) for q in (1, 3, 2)])
    normalise(0)
    scores(1, 3, False)
    scores(1, 1, False)
    stat_pass(0)
    y_last(1)
    scores(1, 2, False)
    reduce_out(1)
    stat_done(0)
    eliminate(40, 8)
    reduce_pass(1)
    eliminate(48, 16)
    residual()
    normalise(1)
    stat_pass(1)
    stat_done(1)
    for c in sent:
        c.wait_send()
    for c in stores:
        c.wait()


N_SENDS = 71


def on_device(dosage, snp_scale, covariates, previous, expression):
    any_spec = pl.BlockSpec(memory_space=pl.ANY)
    vmem_spec = pl.BlockSpec(memory_space=pltpu.VMEM)
    return pl.pallas_call(
        kernel,
        out_shape=(
            jax.ShapeDtypeStruct((ROWS, SNP), BF16),
            jax.ShapeDtypeStruct((SNP, GENES), BF16),
        ),
        in_specs=[any_spec, vmem_spec, any_spec, any_spec, any_spec],
        out_specs=(any_spec, any_spec),
        scratch_shapes=[
            pltpu.VMEM((N, PANEL, GENES), BF16),
            pltpu.VMEM((2, N, PANEL, HALF), BF16),
            pltpu.VMEM((ROWS, SNP), BF16),
            pltpu.VMEM((ROWS, COVS), F32),
            pltpu.VMEM((COVS, AUG), F32),
            pltpu.VMEM((3, SHARE, AUG), F32),
            pltpu.VMEM((3, SHARE, AUG), F32),
            pltpu.VMEM((3, SHARE, AUG), F32),
            pltpu.VMEM((3, SHARE, AUG), F32),
            pltpu.VMEM((N, SHARE, AUG), F32),
            pltpu.VMEM((COVS, AUG), F32),
            pltpu.VMEM((8, GENES), F32),
            pltpu.VMEM((3, 8, GENES), F32),
            pltpu.VMEM((2, HALF, WIDE), F32),
            pltpu.VMEM((2, OWN, WIDE), F32),
            pltpu.VMEM((2, 2, OWN, WIDE), F32),
            pltpu.VMEM((2, N, OWN, GENES), BF16),
            pltpu.VMEM((ROWS, SNP), BF16),
            pltpu.SemaphoreType.DMA((20,)),
            pltpu.SemaphoreType.DMA((N_SENDS,)),
            pltpu.SemaphoreType.DMA((N_SENDS,)),
            pltpu.SemaphoreType.DMA((2 * N + 1,)),
        ],
        compiler_params=pltpu.CompilerParams(
            collective_id=0, has_side_effects=True, vmem_limit_bytes=48 * 1024 * 1024
        ),
    )(dosage, snp_scale[None, :], covariates, previous, expression)


def solution(mesh):
    placed = (
        P(("samp", "gene"), "snp"),
        P("snp"),
        P(("samp", "gene"), None),
        P(("samp", "gene"), "snp"),
        P("samp", "gene"),
    )
    return jax.shard_map(
        on_device,
        mesh=mesh,
        in_specs=placed,
        out_specs=(P(("samp", "gene"), "snp"), P("snp", "gene")),
        check_vma=False,
    )
```

```python
import jax
import jax.numpy as jnp
from jax import lax
from jax.experimental import pallas as pl
from jax.experimental.pallas import tpu as pltpu
from jax.sharding import PartitionSpec as P

F32 = jnp.float32
BF16 = jnp.bfloat16
HIGHEST = lax.Precision.HIGHEST
N = 4
ROWS = 288
CUT = 144
PANEL = N * ROWS
SNP = 256
HALF = 128
GENES = 1280
TILE = 256
TILES = GENES // TILE
OWN = HALF // N
COVS = 64
AUG = 384
SHARE = COVS // N
SAMPLES = 18432


def kernel(
    dosage_hbm, scale_hbm, cov_hbm, prev_hbm, expr_hbm,
    resid_hbm, z_hbm,
    expr, geno, dose, scale, cov_t, part, from_x, from_y, from_z, sums, full, system,
    ysq, from_ysq, acc, xsq, from_acc, from_xsq, stat, resid,
    load_sem, send, recv, store_sem,
):
    s = lax.axis_index("samp")
    gene = lax.axis_index("gene")
    zh, y = gene // N, gene % N

    def peer(axis, step):
        if axis == "x":
            return {"samp": (s + step + N) % N}
        if axis == "y":
            return {"gene": zh * N + (y + step + N) % N}
        return {"gene": ((zh + step + N) % N) * N + y}

    peers = [peer(a, d) for a in "xyz" for d in (1, 2, 3)]
    barrier = pltpu.get_barrier_semaphore()
    for device in peers:
        pl.semaphore_signal(barrier, inc=1, device_id=device, device_id_type=pl.DeviceIdType.MESH)

    loads = [
        pltpu.make_async_copy(cov_hbm, cov_t, load_sem.at[0]),
        pltpu.make_async_copy(dosage_hbm, dose, load_sem.at[1]),
        pltpu.make_async_copy(prev_hbm.at[:, pl.ds(0, HALF)], geno.at[0, 0, pl.ds(0, ROWS)], load_sem.at[2]),
        pltpu.make_async_copy(prev_hbm.at[:, pl.ds(HALF, HALF)], geno.at[1, 0, pl.ds(0, ROWS)], load_sem.at[3]),
        pltpu.make_async_copy(scale_hbm, scale, load_sem.at[20]),
    ]
    for c in loads:
        c.start()
    panels = {}
    for ry in (0, 3, 1, 2):
        for rz in range(N):
            block = ((zh + rz) % N) * N + (y + ry) % N
            c = pltpu.make_async_copy(
                expr_hbm.at[pl.ds(pl.multiple_of(block * ROWS, 16), ROWS)],
                expr.at[ry, pl.ds(rz * ROWS, ROWS)],
                load_sem.at[4 + ry * N + rz],
            )
            c.start()
            panels[ry, rz] = c

    loads[0].wait()
    loads[1].wait()
    part[:, :SNP] = jnp.dot(cov_t[...], dose[...].astype(F32), precision=HIGHEST, preferred_element_type=F32)
    part[:, SNP:] = jnp.zeros((COVS, AUG - SNP), F32)
    part[:, SNP : SNP + COVS] = lax.dot_general(
        cov_t[...], cov_t[...], (((1,), (1,)), ((), ())), precision=HIGHEST, preferred_element_type=F32
    )
    ysq[...] = jnp.zeros((8, GENES), F32)
    loads[2].wait()
    loads[3].wait()
    loads[4].wait()
    pl.semaphore_wait(barrier, len(peers))

    sent = []
    ids = {}

    def push(name, src, dst, axis, step):
        t = len(sent)
        c = pltpu.make_async_remote_copy(
            src_ref=src, dst_ref=dst, send_sem=send.at[t], recv_sem=recv.at[t],
            device_id=peer(axis, step), device_id_type=pl.DeviceIdType.MESH,
        )
        c.start()
        sent.append(c)
        ids[name] = c

    def arrive(*names):
        for name in names:
            ids[name].wait_recv()

    def rows(rz, lo=0, n=ROWS):
        return pl.ds(rz * ROWS + lo, n)

    def z_send(h, *steps):
        for step in steps:
            to = -step % N
            push(("z", h, to), geno.at[h, 0, rows(0)], geno.at[h, 0, rows(to)], "z", step)

    def y_send(h, rz, *steps):
        for step in steps:
            to = -step % N
            push(("y", h, to, rz), geno.at[h, 0, rows(rz)], geno.at[h, to, rows(rz)], "y", step)

    def y_pass(h, rz):
        arrive(("y", h, 3, rz))
        push(("y", h, 2, rz, 0), geno.at[h, 3, rows(rz, 0, CUT)], geno.at[h, 2, rows(rz, 0, CUT)], "y", 1)
        arrive(("y", h, 1, rz))
        push(("y", h, 2, rz, 1), geno.at[h, 1, rows(rz, CUT, CUT)], geno.at[h, 2, rows(rz, CUT, CUT)], "y", -1)

    def y_last(h, *order):
        for rz in order:
            arrive(("y", h, 2, rz, 0), ("y", h, 2, rz, 1))

    def share(q):
        return pl.ds(pl.multiple_of(((s + q) % N) * SHARE, SHARE), SHARE)

    def cov_out():
        for q in (1, 3, 2):
            push(("cx", q), part.at[share(q)], from_x.at[q - 1], "x", q)

    def cov_step(axis_in, landed, base, slot, axis_out, landing, tag):
        arrive(*[(axis_in, q) for q in (1, 3, 2)])
        sums[slot] = base + landed[0] + landed[1] + landed[2]
        for q in (1, 3, 2):
            if landing is None:
                push((tag, q), sums.at[slot], full.at[N - q], axis_out, q)
            else:
                push((tag, q), sums.at[slot], landing.at[q - 1], axis_out, q)

    def square_block(ry, rz):
        panels[ry, rz].wait()

        def body(i, total):
            e = expr[ry, pl.ds(pl.multiple_of(rz * ROWS + i * 16, 16), 16), :].astype(F32)
            e = e * e
            return total + e[:8] + e[8:]

        ysq[...] += lax.fori_loop(0, ROWS // 16, body, jnp.zeros((8, GENES), F32), unroll=2)

    def ysq_out():
        for q in (1, 3, 2):
            push(("q", q), ysq, from_ysq.at[q - 1], "x", q)

    def piece(q):
        return pl.ds(pl.multiple_of(((s + q + N) % N) * OWN, OWN), OWN)

    def scores(h, ry, first=False, last=False):
        lhs = geno[h, ry].T
        f = lhs.astype(F32)
        f = f * f
        squares = f[:, :128]
        for i in range(1, PANEL // 128):
            squares = squares + f[:, i * 128 : (i + 1) * 128]
        xsq[h] = squares if first else xsq[h] + squares
        if last:
            for q in (2, 1, 3):
                push(("x", h, q), xsq.at[h, piece(q)], from_xsq.at[h, q - 1], "x", q)
            for j in range(TILES):
                at = pl.ds(j * TILE, TILE)
                acc[h, :, at] += jnp.dot(lhs, expr[ry, :, at], preferred_element_type=F32)
                for q in (2, 1, 3):
                    push(("r", h, j, q), acc.at[h, piece(q), at], from_acc.at[h, q - 1, :, at], "x", q)
            return

        @pl.loop(0, TILES)
        def _(j):
            at = pl.ds(pl.multiple_of(j * TILE, TILE), TILE)
            d = jnp.dot(lhs, expr[ry, :, at], preferred_element_type=F32)
            acc[h, :, at] = d if first else acc[h, :, at] + d

    stores = []

    def keep(src, dst):
        c = pltpu.make_async_copy(src, dst, store_sem.at[len(stores)])
        c.start()
        stores.append(c)

    def normalise(h):
        y_total = ysq[...] + from_ysq[0] + from_ysq[1] + from_ysq[2]
        y_factor = 1.0 / jnp.sqrt(jnp.sum(y_total, axis=0, keepdims=True) + 1e-6)
        arrive(*[("x", h, q) for q in (1, 3, 2)])
        x_total = xsq[h, piece(0)] + from_xsq[h, 0] + from_xsq[h, 1] + from_xsq[h, 2]
        x_total = jnp.sum(x_total, axis=1, keepdims=True)
        x_factor = jnp.sqrt(F32(SAMPLES)) / jnp.sqrt(x_total + 1e-6)
        out = pl.ds(pl.multiple_of(h * HALF + s * OWN, OWN), OWN)
        for j in range(TILES):
            at = pl.ds(j * TILE, TILE)
            arrive(*[("r", h, j, q) for q in (1, 3, 2)])
            total = acc[h, piece(0), at] + from_acc[h, 0, :, at] + from_acc[h, 1, :, at] + from_acc[h, 2, :, at]
            stat[h, :, at] = (total * x_factor * y_factor[:, j * TILE : (j + 1) * TILE]).astype(BF16)
            for q in (2, 1, 3):
                push(("s", h, j, q), stat.at[h, :, at], z_hbm.at[out, at], "x", q)
            keep(stat.at[h, :, at], z_hbm.at[out, at])

    def stat_done(h):
        for j in range(TILES):
            arrive(*[("s", h, j, q) for q in (1, 3, 2)])

    lane = lax.broadcasted_iota(jnp.int32, (COVS, 128), 1)
    line = lax.broadcasted_iota(jnp.int32, (COVS, AUG), 0)

    def gather_system():
        arrive(*[("cf", q) for q in (1, 3, 2)])
        system[share(0)] = sums[2]
        for q in (1, 2, 3):
            system[share(q)] = full[q]

    def eliminate(start, count):
        def body(k, carry):
            a = system[...]
            row = system[pl.ds(k, 1), :]
            col = jnp.sum(jnp.where(lane == k, a[:, SNP:], 0.0), axis=1, keepdims=True)
            pivot = jnp.sum(jnp.where(lane[:1] == k, row[:, SNP:], 0.0), axis=1, keepdims=True)
            row = row / pivot
            system[...] = jnp.where(line == k, row, a - col * row)
            return carry

        lax.fori_loop(start, start + count, body, 0)

    def residual():
        fit = lax.dot_general(
            cov_t[...], system[:, :SNP], (((0,), (0,)), ((), ())), precision=HIGHEST, preferred_element_type=F32
        )
        resid[...] = ((dose[...].astype(F32) - fit) * scale[...]).astype(BF16)
        keep(resid, resid_hbm)

    z_send(0, 1, -1)
    y_send(0, 0, 1, -1)
    cov_out()
    z_send(0, 2)
    y_send(1, 0, 1, -1)
    z_send(1, 1, -1, 2)
    for rz in range(4):
        square_block(0, rz)
    square_block(3, 0)
    y_pass(0, 0)
    cov_step("cx", from_x, part[share(0)], 0, "y", from_y, "cy")
    arrive(("z", 0, 3))
    y_send(0, 3, 1, -1)
    arrive(("z", 0, 1))
    y_send(0, 1, 1, -1)
    y_pass(1, 0)
    for rz in range(1, 4):
        square_block(3, rz)
    cov_step("cy", from_y, sums[0], 1, "z", from_z, "cz")
    for rz in range(2):
        square_block(1, rz)
    arrive(("z", 0, 2))
    y_send(0, 2, 1, -1)
    scores(0, 0, first=True)
    y_pass(0, 3)
    y_pass(0, 1)
    arrive(("z", 1, 3))
    y_send(1, 3, 1, -1)
    arrive(("z", 1, 1))
    y_send(1, 1, 1, -1)
    for rz in range(2, 4):
        square_block(1, rz)
    y_pass(0, 2)
    for rz in range(4):
        square_block(2, rz)
    ysq_out()
    arrive(("z", 1, 2))
    y_send(1, 2, 1, -1, 2)
    cov_step("cz", from_z, sums[1], 2, "x", None, "cf")
    scores(0, 3)
    scores(0, 1)
    y_last(0, 0, 3, 1, 2)
    scores(0, 2, last=True)
    y_pass(1, 3)
    y_pass(1, 1)
    scores(1, 0, first=True)
    gather_system()
    eliminate(0, 16)
    arrive(*[("y", 1, ry, 2) for ry in (3, 1)])
    scores(1, 3)
    scores(1, 1)
    arrive(*[("q", q) for q in (1, 3, 2)])
    y_last(1, 0, 3, 1)
    arrive(("y", 1, 2, 2))
    scores(1, 2, last=True)
    normalise(0)
    eliminate(16, 16)
    normalise(1)
    eliminate(32, 32)
    residual()
    stat_done(0)
    stat_done(1)
    for c in sent:
        c.wait_send()
    for c in stores:
        c.wait()


N_SENDS = 118
N_STORES = 11


def on_device(dosage, snp_scale, covariates, previous, expression):
    any_spec = pl.BlockSpec(memory_space=pl.ANY)
    return pl.pallas_call(
        kernel,
        out_shape=(
            jax.ShapeDtypeStruct((ROWS, SNP), BF16),
            jax.ShapeDtypeStruct((SNP, GENES), BF16),
        ),
        in_specs=[any_spec] * 5,
        out_specs=(any_spec, any_spec),
        scratch_shapes=[
            pltpu.VMEM((N, PANEL, GENES), BF16),
            pltpu.VMEM((2, N, PANEL, HALF), BF16),
            pltpu.VMEM((ROWS, SNP), BF16),
            pltpu.VMEM((1, SNP), F32),
            pltpu.VMEM((COVS, ROWS), F32),
            pltpu.VMEM((COVS, AUG), F32),
            pltpu.VMEM((3, SHARE, AUG), F32),
            pltpu.VMEM((3, SHARE, AUG), F32),
            pltpu.VMEM((3, SHARE, AUG), F32),
            pltpu.VMEM((3, SHARE, AUG), F32),
            pltpu.VMEM((N, SHARE, AUG), F32),
            pltpu.VMEM((COVS, AUG), F32),
            pltpu.VMEM((8, GENES), F32),
            pltpu.VMEM((3, 8, GENES), F32),
            pltpu.VMEM((2, HALF, GENES), F32),
            pltpu.VMEM((2, HALF, 128), F32),
            pltpu.VMEM((2, 3, OWN, GENES), F32),
            pltpu.VMEM((2, 3, OWN, 128), F32),
            pltpu.VMEM((2, OWN, GENES), BF16),
            pltpu.VMEM((ROWS, SNP), BF16),
            pltpu.SemaphoreType.DMA((21,)),
            pltpu.SemaphoreType.DMA((N_SENDS,)),
            pltpu.SemaphoreType.DMA((N_SENDS,)),
            pltpu.SemaphoreType.DMA((N_STORES,)),
        ],
        compiler_params=pltpu.CompilerParams(
            collective_id=0, has_side_effects=True, vmem_limit_bytes=62 * 1024 * 1024
        ),
    )(dosage, snp_scale[None, :], covariates.T, previous, expression)


def solution(mesh):
    placed = (
        P(("samp", "gene"), "snp"),
        P("snp"),
        P(("samp", "gene"), None),
        P(("samp", "gene"), "snp"),
        P("samp", "gene"),
    )
    return jax.shard_map(
        on_device,
        mesh=mesh,
        in_specs=placed,
        out_specs=(P(("samp", "gene"), "snp"), P("snp", "gene")),
        check_vma=False,
    )
```

```python
import jax
import jax.numpy as jnp
from jax import lax
from jax.experimental import pallas as pl
from jax.experimental.pallas import tpu as pltpu
from jax.sharding import PartitionSpec as P

F32 = jnp.float32
BF16 = jnp.bfloat16
HIGHEST = lax.Precision.HIGHEST
N = 4
ROWS = 288
PACK = ROWS // 2
CUT = 80
LINES = N * PACK
PANEL = N * ROWS
SNP = 256
CHUNK = 64
CHUNKS = SNP // CHUNK
GENES = 1280
OWN = CHUNK // N
SPANS = (
    ((0, 512), (512, 768)),
    ((0, 1280),),
    ((0, 1280),),
    ((0, 256), (256, 256), (512, 256), (768, 256), (1024, 256)),
)
COVS = 64
AUG = 384
SHARE = COVS // N
SAMPLES = 18432

ORDER = (
    ("z", 0), ("y", 0, 0), ("y", 2, 0), ("z", 1), ("cov_out",), ("y", 1, 0),
    ("z", 2), ("square", 3), ("square", 0), ("cov", 0), ("y", 0, 1), ("y", 0, 2),
    ("y", 0, 3), ("square", 1), ("cov", 1), ("square", 2), ("y", 1, 1), ("z", 3),
    ("scores", 1, 0), ("ysq",), ("y", 1, 2), ("scores", 0, 0), ("y", 1, 3), ("y", 2, 3),
    ("scores", 0, 3), ("scores", 2, 0), ("scores", 0, 1), ("cov", 2), ("y", 2, 2), ("y", 2, 1),
    ("scores", 0, 2), ("scores", 1, 3), ("scores", 1, 1), ("y", 3, 0), ("y_factors",), ("y", 3, 1),
    ("y", 3, 2), ("scores", 1, 2), ("solve_in",), ("y", 3, 3), ("solve", 0), ("scores", 2, 3),
    ("scores", 2, 1), ("norm", 0), ("scores", 2, 2), ("solve", 1), ("solve", 2), ("scores", 3, 0),
    ("norm", 1), ("scores", 3, 1), ("scores", 3, 3), ("scores", 3, 2), ("solve", 3), ("solve", 4),
    ("norm", 2), ("solve", 5), ("solve", 6), ("norm", 3), ("solve", 7), ("resid",),
)
DIRECT = {(0, 0), (0, 1), (0, 2), (0, 3), (1, 0), (1, 1), (1, 2), (1, 3), (2, 0), (2, 1), (2, 2), (2, 3), (3, 0), (3, 1), (3, 2), (3, 3)}


def kernel(
    dosage_hbm, scale_hbm, cov_hbm, prev_hbm, expr_hbm,
    resid_hbm, z_hbm,
    expr, geno, prev, dose, scale, cov_t, part, from_x, from_y, from_z, sums, full, system,
    ysq, from_ysq, y_factor, acc, xsq, from_acc, stat, resid,
    load_sem, send, recv, store_sem,
):
    s = lax.axis_index("samp")
    gene = lax.axis_index("gene")
    zh, y = gene // N, gene % N

    def peer(axis, step):
        if axis == "x":
            return {"samp": (s + step + N) % N}
        if axis == "y":
            return {"gene": zh * N + (y + step + N) % N}
        return {"gene": ((zh + step + N) % N) * N + y}

    peers = [peer(a, d) for a in "xyz" for d in (1, 2, 3)]
    barrier = pltpu.get_barrier_semaphore()
    for device in peers:
        pl.semaphore_signal(barrier, inc=1, device_id=device, device_id_type=pl.DeviceIdType.MESH)

    loads = [
        pltpu.make_async_copy(prev_hbm, prev, load_sem.at[0]),
        pltpu.make_async_copy(cov_hbm, cov_t, load_sem.at[1]),
        pltpu.make_async_copy(dosage_hbm, dose, load_sem.at[2]),
        pltpu.make_async_copy(scale_hbm, scale, load_sem.at[3]),
    ]
    for c in loads:
        c.start()
    panels = {}
    for ry in (0, 3, 1, 2):
        for rz in range(N):
            block = ((zh + rz) % N) * N + (y + ry) % N
            for half in (0, 1):
                start = pl.multiple_of(block * ROWS + half * PACK, 16)
                c = pltpu.make_async_copy(
                    expr_hbm.at[pl.ds(start, PACK)],
                    expr.at[ry, pl.ds(half * LINES + rz * PACK, PACK)],
                    load_sem.at[4 + (ry * N + rz) * 2 + half],
                )
                c.start()
                panels[ry, rz, half] = c

    loads[0].wait()
    left = lax.broadcasted_iota(jnp.int32, (PACK, 2 * CHUNK), 1) < CHUNK
    spot = lax.broadcasted_iota(jnp.int32, (COVS, AUG - SNP), 1)
    squares = jnp.zeros((COVS, AUG - SNP), F32)
    for c in range(CHUNKS):
        at = pl.ds(c // 2 * 2 * CHUNK, 2 * CHUNK)
        top, bottom = prev[:PACK, at].astype(F32), prev[PACK:, at].astype(F32)
        if c % 2 == 0:
            both = jnp.where(left, top, pltpu.roll(bottom, CHUNK, 1))
        else:
            both = jnp.where(left, pltpu.roll(top, CHUNK, 1), bottom)
        geno[c, 0, :PACK] = both.astype(BF16)
        turned = both.T
        column = jnp.sum(turned * turned, axis=1, keepdims=True)
        squares = jnp.where(spot == COVS + c, column[:CHUNK] + column[CHUNK:], squares)

    loads[1].wait()
    loads[2].wait()
    part[:, :SNP] = jnp.dot(cov_t[...], dose[...].astype(F32), precision=HIGHEST, preferred_element_type=F32)
    part[:, SNP:] = squares
    part[:, SNP : SNP + COVS] = lax.dot_general(
        cov_t[...], cov_t[...], (((1,), (1,)), ((), ())), precision=HIGHEST, preferred_element_type=F32
    )
    ysq[...] = jnp.zeros((1, GENES), F32)
    loads[3].wait()
    pl.semaphore_wait(barrier, len(peers))

    sent = []
    ids = {}

    def push(name, src, dst, axis, step):
        t = len(sent)
        c = pltpu.make_async_remote_copy(
            src_ref=src, dst_ref=dst, send_sem=send.at[t], recv_sem=recv.at[t],
            device_id=peer(axis, step), device_id_type=pl.DeviceIdType.MESH,
        )
        c.start()
        sent.append(c)
        ids[name] = c

    landed = set()

    def arrive(*names):
        for name in names:
            if name not in landed:
                ids[name].wait_recv()
                landed.add(name)

    def rows(rz, lo=0, n=PACK):
        return pl.ds(rz * PACK + lo, n)

    def z_send(c):
        for step in (1, -1, 2):
            to = -step % N
            push(("z", c, to), geno.at[c, 0, rows(0)], geno.at[c, 0, rows(to)], "z", step)

    def y_go(c, rz):
        if rz:
            arrive(("z", c, rz))
        for step in (1, -1, 2) if (c, rz) in DIRECT else (1, -1):
            to = -step % N
            push(("y", c, to, rz), geno.at[c, 0, rows(rz)], geno.at[c, to, rows(rz)], "y", step)

    def y_pass(c, rz):
        arrive(("y", c, 3, rz))
        push(("y", c, 2, rz, 0), geno.at[c, 3, rows(rz, 0, CUT)], geno.at[c, 2, rows(rz, 0, CUT)], "y", 1)
        arrive(("y", c, 1, rz))
        push(("y", c, 2, rz, 1), geno.at[c, 1, rows(rz, CUT, PACK - CUT)], geno.at[c, 2, rows(rz, CUT, PACK - CUT)], "y", -1)

    def panel_arrive(c, ry):
        for rz in (0, 3, 1, 2):
            if ry == 0 and rz:
                arrive(("z", c, rz))
            elif ry in (1, 3) or (ry and (c, rz) in DIRECT):
                arrive(("y", c, ry, rz))
            elif ry:
                arrive(("y", c, 2, rz, 0), ("y", c, 2, rz, 1))

    def share(q):
        return pl.ds(pl.multiple_of(((s + q) % N) * SHARE, SHARE), SHARE)

    def cov_out():
        for q in (1, 3, 2):
            push(("cx", q), part.at[share(q)], from_x.at[q - 1], "x", q)

    def cov(i):
        tag, landing, base = (("cx", from_x, part.at[share(0)]), ("cy", from_y, sums.at[0]), ("cz", from_z, sums.at[1]))[i]
        arrive(*[(tag, q) for q in (1, 3, 2)])
        sums[i] = base[...] + landing[0] + landing[1] + landing[2]
        for q in (1, 3, 2):
            if i == 0:
                push(("cy", q), sums.at[0], from_y.at[q - 1], "y", q)
            elif i == 1:
                push(("cz", q), sums.at[1], from_z.at[q - 1], "z", q)
            else:
                push(("cf", q), sums.at[2], full.at[N - q], "x", q)

    seen = set()

    def square(ry):
        total = jnp.zeros((8, GENES), F32)
        for half in (0, 1):
            for rz in range(N):
                if (ry, rz) not in seen:
                    panels[ry, rz, half].wait()

            def body(i, total):
                e = expr[ry, pl.ds(pl.multiple_of(half * LINES + i * 16, 16), 16), :].astype(F32)
                e = e * e
                return total + e[:8] + e[8:]

            total = lax.fori_loop(0, LINES // 16, body, total, unroll=3)
        seen.update((ry, rz) for rz in range(N))
        ysq[...] += jnp.sum(total, axis=0, keepdims=True)

    def ysq_out():
        for q in (1, 3, 2):
            push(("q", q), ysq, from_ysq.at[q - 1], "x", q)

    def piece(q):
        return pl.ds(pl.multiple_of(((s + q) % N) * OWN, OWN), OWN)

    begun = set()

    def scores(c, ry):
        first, last = c not in begun, ry == 2
        begun.add(c)
        for rz in range(N):
            for half in (0, 1):
                if (ry, rz) not in seen:
                    panels[ry, rz, half].wait()
            seen.add((ry, rz))
        panel_arrive(c, ry)
        packed = geno[c, ry].astype(F32)
        lhs = jnp.concatenate([packed, pltpu.roll(packed, CHUNK, 1)], axis=0).astype(BF16).T[:CHUNK]
        for j, (start, size) in enumerate(SPANS[c] if last else SPANS[3]):
            at = pl.ds(start, size)
            d = jnp.dot(lhs, expr[ry, :, at], preferred_element_type=F32)
            acc[c, :, at] = d if first else acc[c, :, at] + d
            if last:
                for q in (2, 1, 3):
                    push(("r", c, j, q), acc.at[c, piece(q), at], from_acc.at[c, q - 1, :, at], "x", q)

    stores = []

    def keep(src, dst):
        c = pltpu.make_async_copy(src, dst, store_sem.at[len(stores)])
        c.start()
        stores.append(c)

    def normalise(c):
        x_total = xsq[piece(0), :][:, COVS + c : COVS + c + 1]
        x_factor = jnp.sqrt(F32(SAMPLES)) / jnp.sqrt(x_total + 1e-6)
        out = pl.ds(pl.multiple_of(c * CHUNK + s * OWN, OWN), OWN)
        for j, (start, size) in enumerate(SPANS[c]):
            at = pl.ds(start, size)
            arrive(*[("r", c, j, q) for q in (1, 3, 2)])
            total = acc[c, piece(0), at] + from_acc[c, 0, :, at] + from_acc[c, 1, :, at] + from_acc[c, 2, :, at]
            stat[c, :, at] = (total * x_factor * y_factor[:, at]).astype(BF16)
            for q in (2, 1, 3):
                push(("s", c, j, q), stat.at[c, :, at], z_hbm.at[out, at], "x", q)
            keep(stat.at[c, :, at], z_hbm.at[out, at])

    def y_factors():
        arrive(*[("q", q) for q in (1, 3, 2)])
        y_total = ysq[...] + from_ysq[0] + from_ysq[1] + from_ysq[2]
        y_factor[...] = 1.0 / jnp.sqrt(y_total + 1e-6)

    def stat_done(c):
        for j in range(len(SPANS[c])):
            arrive(*[("s", c, j, q) for q in (1, 3, 2)])

    lane = lax.broadcasted_iota(jnp.int32, (COVS, 128), 1)
    line = lax.broadcasted_iota(jnp.int32, (COVS, AUG), 0)

    def solve_in():
        arrive(*[("cf", q) for q in (1, 3, 2)])
        system[share(0)] = sums[2]
        for q in (1, 2, 3):
            system[share(q)] = full[q]
        xsq[...] = system[:, SNP:]

    def eliminate(i):
        start, count = i * 8, 8

        def body(k, carry):
            a = system[...]
            row = system[pl.ds(k, 1), :]
            col = jnp.sum(jnp.where(lane == k, a[:, SNP:], 0.0), axis=1, keepdims=True)
            pivot = jnp.sum(jnp.where(lane[:1] == k, row[:, SNP:], 0.0), axis=1, keepdims=True)
            row = row / pivot
            system[...] = jnp.where(line == k, row, a - col * row)
            return carry

        lax.fori_loop(start, start + count, body, 0)

    def residual():
        fit = lax.dot_general(
            cov_t[...], system[:, :SNP], (((0,), (0,)), ((), ())), precision=HIGHEST, preferred_element_type=F32
        )
        resid[...] = ((dose[...].astype(F32) - fit) * scale[...]).astype(BF16)
        keep(resid, resid_hbm)

    steps = {
        "z": z_send, "y": y_go, "pass": y_pass, "cov_out": cov_out, "cov": cov, "square": square, "ysq": ysq_out,
        "y_factors": y_factors, "solve_in": solve_in, "solve": eliminate, "resid": residual, "scores": scores, "norm": normalise,
    }
    for name, *at in ORDER:
        steps[name](*at)
    for c in range(CHUNKS):
        stat_done(c)
    for c in sent:
        c.wait_send()
    for c in stores:
        c.wait()


N_SENDS = 129
N_STORES = 10


def on_device(dosage, snp_scale, covariates, previous, expression):
    any_spec = pl.BlockSpec(memory_space=pl.ANY)
    return pl.pallas_call(
        kernel,
        out_shape=(
            jax.ShapeDtypeStruct((ROWS, SNP), BF16),
            jax.ShapeDtypeStruct((SNP, GENES), BF16),
        ),
        in_specs=[any_spec] * 5,
        out_specs=(any_spec, any_spec),
        scratch_shapes=[
            pltpu.VMEM((N, PANEL, GENES), BF16),
            pltpu.VMEM((CHUNKS, N, LINES, 2 * CHUNK), BF16),
            pltpu.VMEM((ROWS, SNP), BF16),
            pltpu.VMEM((ROWS, SNP), BF16),
            pltpu.VMEM((1, SNP), F32),
            pltpu.VMEM((COVS, ROWS), F32),
            pltpu.VMEM((COVS, AUG), F32),
            pltpu.VMEM((3, SHARE, AUG), F32),
            pltpu.VMEM((3, SHARE, AUG), F32),
            pltpu.VMEM((3, SHARE, AUG), F32),
            pltpu.VMEM((3, SHARE, AUG), F32),
            pltpu.VMEM((N, SHARE, AUG), F32),
            pltpu.VMEM((COVS, AUG), F32),
            pltpu.VMEM((1, GENES), F32),
            pltpu.VMEM((3, 1, GENES), F32),
            pltpu.VMEM((1, GENES), F32),
            pltpu.VMEM((CHUNKS, CHUNK, GENES), F32),
            pltpu.VMEM((COVS, AUG - SNP), F32),
            pltpu.VMEM((CHUNKS, 3, OWN, GENES), F32),
            pltpu.VMEM((CHUNKS, OWN, GENES), BF16),
            pltpu.VMEM((ROWS, SNP), BF16),
            pltpu.SemaphoreType.DMA((36,)),
            pltpu.SemaphoreType.DMA((N_SENDS,)),
            pltpu.SemaphoreType.DMA((N_SENDS,)),
            pltpu.SemaphoreType.DMA((N_STORES,)),
        ],
        compiler_params=pltpu.CompilerParams(
            collective_id=0, has_side_effects=True, vmem_limit_bytes=62 * 1024 * 1024
        ),
    )(dosage, snp_scale[None, :], covariates.T, previous, expression)


def solution(mesh):
    placed = (
        P(("samp", "gene"), "snp"),
        P("snp"),
        P(("samp", "gene"), None),
        P(("samp", "gene"), "snp"),
        P("samp", "gene"),
    )
    return jax.shard_map(
        on_device,
        mesh=mesh,
        in_specs=placed,
        out_specs=(P(("samp", "gene"), "snp"), P("snp", "gene")),
        check_vma=False,
    )
```

```python
import jax
import jax.numpy as jnp
from jax import lax
from jax.experimental import pallas as pl
from jax.experimental.pallas import tpu as pltpu
from jax.sharding import PartitionSpec as P

F32 = jnp.float32
BF16 = jnp.bfloat16
HIGHEST = lax.Precision.HIGHEST
N = 4
ROWS = 288
PACK = ROWS // 2
CUT = 80
LINES = N * PACK
PANEL = N * ROWS
SNP = 256
CHUNK = 64
CHUNKS = SNP // CHUNK
GENES = 1280
OWN = CHUNK // N
SPANS = (
    ((0, 512), (512, 768)),
    ((0, 1280),),
    ((0, 1280),),
    ((0, 256), (256, 256), (512, 256), (768, 256), (1024, 256)),
)
COVS = 64
AUG = 384
SHARE = COVS // N
SAMPLES = 18432

ORDER = (
    ("z", 0), ("y", 0, 0), ("y", 1, 0), ("y", 2, 0), ("cov_out",), ("square", 0),
    ("square", 3), ("square", 2), ("z", 1), ("cov", 0), ("y", 0, 3), ("z", 2),
    ("y", 0, 1), ("cov", 1), ("y", 0, 2), ("square", 1), ("scores", 0, 0), ("y", 1, 2),
    ("y", 1, 3), ("y", 1, 1), ("scores", 1, 0), ("ysq",), ("z", 3), ("scores", 0, 1),
    ("scores", 0, 3), ("y", 2, 1), ("cov", 2), ("y", 2, 2), ("y", 2, 3), ("y_factors",),
    ("scores", 0, 2), ("scores", 2, 0), ("scores", 1, 1), ("scores", 1, 3), ("y", 3, 3), ("y", 3, 0),
    ("solve_in",), ("y", 3, 1), ("y", 3, 2), ("scores", 1, 2), ("solve", 0), ("scores", 3, 0),
    ("scores", 2, 3), ("norm", 0), ("scores", 2, 1), ("scores", 2, 2), ("solve", 1), ("solve", 2),
    ("norm", 1), ("scores", 3, 3), ("scores", 3, 1), ("scores", 3, 2), ("solve", 3), ("solve", 4),
    ("solve", 5), ("norm", 2), ("solve", 6), ("norm", 3), ("solve", 7), ("resid",),
)
DIRECT = {(0, 0), (0, 1), (0, 2), (0, 3), (1, 0), (1, 1), (1, 2), (1, 3), (2, 0), (2, 1), (2, 2), (2, 3), (3, 0), (3, 1), (3, 2), (3, 3)}


def kernel(
    dosage_hbm, scale_hbm, cov_hbm, prev_hbm, expr_hbm,
    resid_hbm, z_hbm,
    expr, geno, prev, dose, scale, cov_t, part, from_x, from_y, from_z, sums, full, system,
    ysq, from_ysq, y_factor, acc, xsq, from_acc, stat, resid,
    load_sem, send, recv, store_sem,
):
    s = lax.axis_index("samp")
    gene = lax.axis_index("gene")
    zh, y = gene // N, gene % N

    def peer(axis, step):
        if axis == "x":
            return {"samp": (s + step + N) % N}
        if axis == "y":
            return {"gene": zh * N + (y + step + N) % N}
        return {"gene": ((zh + step + N) % N) * N + y}

    peers = [peer(a, d) for a in "xyz" for d in (1, 2, 3)]
    barrier = pltpu.get_barrier_semaphore()
    for device in peers:
        pl.semaphore_signal(barrier, inc=1, device_id=device, device_id_type=pl.DeviceIdType.MESH)

    loads = [
        pltpu.make_async_copy(prev_hbm, prev, load_sem.at[0]),
        pltpu.make_async_copy(cov_hbm, cov_t, load_sem.at[1]),
        pltpu.make_async_copy(dosage_hbm, dose, load_sem.at[2]),
        pltpu.make_async_copy(scale_hbm, scale, load_sem.at[3]),
    ]
    for c in loads:
        c.start()
    panels = {}
    for ry in (0, 3, 1, 2):
        for rz in range(N):
            block = ((zh + rz) % N) * N + (y + ry) % N
            for half in (0, 1):
                start = pl.multiple_of(block * ROWS + half * PACK, 16)
                c = pltpu.make_async_copy(
                    expr_hbm.at[pl.ds(start, PACK)],
                    expr.at[ry, pl.ds(half * LINES + rz * PACK, PACK)],
                    load_sem.at[4 + (ry * N + rz) * 2 + half],
                )
                c.start()
                panels[ry, rz, half] = c

    loads[0].wait()
    left = lax.broadcasted_iota(jnp.int32, (PACK, 2 * CHUNK), 1) < CHUNK
    spot = lax.broadcasted_iota(jnp.int32, (COVS, AUG - SNP), 1)
    squares = jnp.zeros((COVS, AUG - SNP), F32)
    for c in range(CHUNKS):
        at = pl.ds(c // 2 * 2 * CHUNK, 2 * CHUNK)
        top, bottom = prev[:PACK, at].astype(F32), prev[PACK:, at].astype(F32)
        if c % 2 == 0:
            both = jnp.where(left, top, pltpu.roll(bottom, CHUNK, 1))
        else:
            both = jnp.where(left, pltpu.roll(top, CHUNK, 1), bottom)
        geno[c, 0, :PACK] = both.astype(BF16)
        turned = both.T
        column = jnp.sum(turned * turned, axis=1, keepdims=True)
        squares = jnp.where(spot == COVS + c, column[:CHUNK] + column[CHUNK:], squares)

    loads[1].wait()
    loads[2].wait()
    part[:, :SNP] = jnp.dot(cov_t[...], dose[...].astype(F32), precision=HIGHEST, preferred_element_type=F32)
    part[:, SNP:] = squares
    part[:, SNP : SNP + COVS] = lax.dot_general(
        cov_t[...], cov_t[...], (((1,), (1,)), ((), ())), precision=HIGHEST, preferred_element_type=F32
    )
    ysq[...] = jnp.zeros((1, GENES), F32)
    loads[3].wait()
    pl.semaphore_wait(barrier, len(peers))

    sent = []
    ids = {}

    def push(name, src, dst, axis, step):
        t = len(sent)
        c = pltpu.make_async_remote_copy(
            src_ref=src, dst_ref=dst, send_sem=send.at[t], recv_sem=recv.at[t],
            device_id=peer(axis, step), device_id_type=pl.DeviceIdType.MESH,
        )
        c.start()
        sent.append(c)
        ids[name] = c

    landed = set()

    def arrive(*names):
        for name in names:
            if name not in landed:
                ids[name].wait_recv()
                landed.add(name)

    def rows(rz, lo=0, n=PACK):
        return pl.ds(rz * PACK + lo, n)

    def z_send(c):
        for step in (1, -1, 2):
            to = -step % N
            push(("z", c, to), geno.at[c, 0, rows(0)], geno.at[c, 0, rows(to)], "z", step)

    def y_go(c, rz):
        if rz:
            arrive(("z", c, rz))
        for step in (1, -1, 2) if (c, rz) in DIRECT else (1, -1):
            to = -step % N
            push(("y", c, to, rz), geno.at[c, 0, rows(rz)], geno.at[c, to, rows(rz)], "y", step)

    def y_pass(c, rz):
        arrive(("y", c, 3, rz))
        push(("y", c, 2, rz, 0), geno.at[c, 3, rows(rz, 0, CUT)], geno.at[c, 2, rows(rz, 0, CUT)], "y", 1)
        arrive(("y", c, 1, rz))
        push(("y", c, 2, rz, 1), geno.at[c, 1, rows(rz, CUT, PACK - CUT)], geno.at[c, 2, rows(rz, CUT, PACK - CUT)], "y", -1)

    def panel_arrive(c, ry):
        for rz in (0, 3, 1, 2):
            if ry == 0 and rz:
                arrive(("z", c, rz))
            elif ry in (1, 3) or (ry and (c, rz) in DIRECT):
                arrive(("y", c, ry, rz))
            elif ry:
                arrive(("y", c, 2, rz, 0), ("y", c, 2, rz, 1))

    def share(q):
        return pl.ds(pl.multiple_of(((s + q) % N) * SHARE, SHARE), SHARE)

    def cov_out():
        for q in (1, 3, 2):
            push(("cx", q), part.at[share(q)], from_x.at[q - 1], "x", q)

    def cov(i):
        tag, landing, base = (("cx", from_x, part.at[share(0)]), ("cy", from_y, sums.at[0]), ("cz", from_z, sums.at[1]))[i]
        arrive(*[(tag, q) for q in (1, 3, 2)])
        sums[i] = base[...] + landing[0] + landing[1] + landing[2]
        for q in (1, 3, 2):
            if i == 0:
                push(("cy", q), sums.at[0], from_y.at[q - 1], "y", q)
            elif i == 1:
                push(("cz", q), sums.at[1], from_z.at[q - 1], "z", q)
            else:
                push(("cf", q), sums.at[2], full.at[N - q], "x", q)

    seen = set()

    def square(ry):
        total = jnp.zeros((8, GENES), F32)
        for half in (0, 1):
            for rz in range(N):
                if (ry, rz) not in seen:
                    panels[ry, rz, half].wait()

            def body(i, total):
                e = expr[ry, pl.ds(pl.multiple_of(half * LINES + i * 16, 16), 16), :].astype(F32)
                e = e * e
                return total + e[:8] + e[8:]

            total = lax.fori_loop(0, LINES // 16, body, total, unroll=6)
        seen.update((ry, rz) for rz in range(N))
        ysq[...] += jnp.sum(total, axis=0, keepdims=True)

    def ysq_out():
        for q in (1, 3, 2):
            push(("q", q), ysq, from_ysq.at[q - 1], "x", q)

    def piece(q):
        return pl.ds(pl.multiple_of(((s + q) % N) * OWN, OWN), OWN)

    begun = set()

    def scores(c, ry):
        first, last = c not in begun, ry == 2
        begun.add(c)
        for rz in range(N):
            for half in (0, 1):
                if (ry, rz) not in seen:
                    panels[ry, rz, half].wait()
            seen.add((ry, rz))
        panel_arrive(c, ry)
        turned = geno[c, ry].T
        lhs = jnp.concatenate([turned[:CHUNK], turned[CHUNK:]], axis=1)
        for j, (start, size) in enumerate(SPANS[c] if last else SPANS[3]):
            at = pl.ds(start, size)
            d = jnp.dot(lhs, expr[ry, :, at], preferred_element_type=F32)
            acc[c, :, at] = d if first else acc[c, :, at] + d
            if last:
                for q in (2, 1, 3):
                    push(("r", c, j, q), acc.at[c, piece(q), at], from_acc.at[c, q - 1, :, at], "x", q)

    stores = []

    def keep(src, dst):
        c = pltpu.make_async_copy(src, dst, store_sem.at[len(stores)])
        c.start()
        stores.append(c)

    def normalise(c):
        x_total = xsq[piece(0), :][:, COVS + c : COVS + c + 1]
        x_factor = jnp.sqrt(F32(SAMPLES)) / jnp.sqrt(x_total + 1e-6)
        out = pl.ds(pl.multiple_of(c * CHUNK + s * OWN, OWN), OWN)
        for j, (start, size) in enumerate(SPANS[c]):
            at = pl.ds(start, size)
            arrive(*[("r", c, j, q) for q in (1, 3, 2)])
            total = acc[c, piece(0), at] + from_acc[c, 0, :, at] + from_acc[c, 1, :, at] + from_acc[c, 2, :, at]
            stat[c, :, at] = (total * x_factor * y_factor[:, at]).astype(BF16)
            for q in (2, 1, 3):
                push(("s", c, j, q), stat.at[c, :, at], z_hbm.at[out, at], "x", q)
            keep(stat.at[c, :, at], z_hbm.at[out, at])

    def y_factors():
        arrive(*[("q", q) for q in (1, 3, 2)])
        y_total = ysq[...] + from_ysq[0] + from_ysq[1] + from_ysq[2]
        y_factor[...] = 1.0 / jnp.sqrt(y_total + 1e-6)

    def stat_done(c):
        for j in range(len(SPANS[c])):
            arrive(*[("s", c, j, q) for q in (1, 3, 2)])

    lane = lax.broadcasted_iota(jnp.int32, (COVS, 128), 1)
    line = lax.broadcasted_iota(jnp.int32, (COVS, AUG), 0)

    def solve_in():
        arrive(*[("cf", q) for q in (1, 3, 2)])
        system[share(0)] = sums[2]
        for q in (1, 2, 3):
            system[share(q)] = full[q]
        xsq[...] = system[:, SNP:]

    def eliminate(i):
        start, count = i * 8, 8

        def body(k, carry):
            a = system[...]
            row = system[pl.ds(k, 1), :]
            col = jnp.sum(jnp.where(lane == k, a[:, SNP:], 0.0), axis=1, keepdims=True)
            pivot = jnp.sum(jnp.where(lane[:1] == k, row[:, SNP:], 0.0), axis=1, keepdims=True)
            row = row / pivot
            system[...] = jnp.where(line == k, row, a - col * row)
            return carry

        lax.fori_loop(start, start + count, body, 0)

    def residual():
        fit = lax.dot_general(
            cov_t[...], system[:, :SNP], (((0,), (0,)), ((), ())), precision=HIGHEST, preferred_element_type=F32
        )
        resid[...] = ((dose[...].astype(F32) - fit) * scale[...]).astype(BF16)
        keep(resid, resid_hbm)

    steps = {
        "z": z_send, "y": y_go, "pass": y_pass, "cov_out": cov_out, "cov": cov, "square": square, "ysq": ysq_out,
        "y_factors": y_factors, "solve_in": solve_in, "solve": eliminate, "resid": residual, "scores": scores, "norm": normalise,
    }
    for name, *at in ORDER:
        steps[name](*at)
    for c in range(CHUNKS):
        stat_done(c)
    for c in sent:
        c.wait_send()
    for c in stores:
        c.wait()


N_SENDS = 129
N_STORES = 10


def keep_all(resid_in, z_in, resid_out, z_out, resid_held, z_held, in_sem, out_sem):
    ways = [(resid_in, resid_held, resid_out)]
    for i in range(N):
        at = pl.ds(i * CHUNK, CHUNK)
        ways.append((z_in.at[at], z_held.at[at], z_out.at[at]))
    ins = [pltpu.make_async_copy(a, b, in_sem.at[i]) for i, (a, b, _) in enumerate(ways)]
    outs = [pltpu.make_async_copy(b, c, out_sem.at[i]) for i, (_, b, c) in enumerate(ways)]
    for copy in ins:
        copy.start()
    for first, then in zip(ins, outs):
        first.wait()
        then.start()
    for copy in outs:
        copy.wait()


def on_device(dosage, snp_scale, covariates, previous, expression):
    any_spec = pl.BlockSpec(memory_space=pl.ANY)
    resid, z = pl.pallas_call(
        kernel,
        out_shape=(
            jax.ShapeDtypeStruct((ROWS, SNP), BF16),
            jax.ShapeDtypeStruct((SNP, GENES), BF16),
        ),
        in_specs=[any_spec] * 5,
        out_specs=(any_spec, any_spec),
        scratch_shapes=[
            pltpu.VMEM((N, PANEL, GENES), BF16),
            pltpu.VMEM((CHUNKS, N, LINES, 2 * CHUNK), BF16),
            pltpu.VMEM((ROWS, SNP), BF16),
            pltpu.VMEM((ROWS, SNP), BF16),
            pltpu.VMEM((1, SNP), F32),
            pltpu.VMEM((COVS, ROWS), F32),
            pltpu.VMEM((COVS, AUG), F32),
            pltpu.VMEM((3, SHARE, AUG), F32),
            pltpu.VMEM((3, SHARE, AUG), F32),
            pltpu.VMEM((3, SHARE, AUG), F32),
            pltpu.VMEM((3, SHARE, AUG), F32),
            pltpu.VMEM((N, SHARE, AUG), F32),
            pltpu.VMEM((COVS, AUG), F32),
            pltpu.VMEM((1, GENES), F32),
            pltpu.VMEM((3, 1, GENES), F32),
            pltpu.VMEM((1, GENES), F32),
            pltpu.VMEM((CHUNKS, CHUNK, GENES), F32),
            pltpu.VMEM((COVS, AUG - SNP), F32),
            pltpu.VMEM((CHUNKS, 3, OWN, GENES), F32),
            pltpu.VMEM((CHUNKS, OWN, GENES), BF16),
            pltpu.VMEM((ROWS, SNP), BF16),
            pltpu.SemaphoreType.DMA((36,)),
            pltpu.SemaphoreType.DMA((N_SENDS,)),
            pltpu.SemaphoreType.DMA((N_SENDS,)),
            pltpu.SemaphoreType.DMA((N_STORES,)),
        ],
        compiler_params=pltpu.CompilerParams(
            collective_id=0, has_side_effects=True, vmem_limit_bytes=62 * 1024 * 1024
        ),
    )(dosage, snp_scale[None, :], covariates.T, previous, expression)
    return pl.pallas_call(
        keep_all,
        out_shape=(
            jax.ShapeDtypeStruct((ROWS, SNP), BF16),
            jax.ShapeDtypeStruct((SNP, GENES), BF16),
        ),
        in_specs=[any_spec] * 2,
        out_specs=(any_spec, any_spec),
        scratch_shapes=[
            pltpu.VMEM((ROWS, SNP), BF16),
            pltpu.VMEM((SNP, GENES), BF16),
            pltpu.SemaphoreType.DMA((N + 1,)),
            pltpu.SemaphoreType.DMA((N + 1,)),
        ],
        compiler_params=pltpu.CompilerParams(vmem_limit_bytes=62 * 1024 * 1024),
    )(resid, z)


def solution(mesh):
    placed = (
        P(("samp", "gene"), "snp"),
        P("snp"),
        P(("samp", "gene"), None),
        P(("samp", "gene"), "snp"),
        P("samp", "gene"),
    )
    return jax.shard_map(
        on_device,
        mesh=mesh,
        in_specs=placed,
        out_specs=(P(("samp", "gene"), "snp"), P("snp", "gene")),
        check_vma=False,
    )
```

```python
import jax
import jax.numpy as jnp
from jax import lax
from jax.experimental import pallas as pl
from jax.experimental.pallas import tpu as pltpu
from jax.sharding import PartitionSpec as P

F32 = jnp.float32
BF16 = jnp.bfloat16
HIGHEST = lax.Precision.HIGHEST
N = 4
ROWS = 288
PACK = ROWS // 2
CUT = 80
LINES = N * PACK
PANEL = N * ROWS
SNP = 256
CHUNK = 64
CHUNKS = SNP // CHUNK
GENES = 1280
OWN = CHUNK // N
SPANS = (
    ((0, 512), (512, 768)),
    ((0, 1280),),
    ((0, 1280),),
    ((0, 256), (256, 256), (512, 256), (768, 256), (1024, 256)),
)
COVS = 64
AUG = 384
SHARE = COVS // N
SAMPLES = 18432

ORDER = (
    ("z", 1), ("y", 2, 0), ("cov_out",), ("y", 1, 0), ("square", 3), ("square", 2),
    ("y", 0, 0), ("z", 2), ("cov", 0), ("square", 1), ("y", 1, 1), ("y", 1, 3),
    ("y", 1, 2), ("z", 0), ("square", 0), ("cov", 1), ("y", 2, 2), ("ysq",),
    ("scores", 2, 0), ("y", 2, 1), ("scores", 1, 0), ("y", 2, 3), ("z", 3), ("y_factors",),
    ("scores", 1, 3), ("scores", 1, 1), ("y", 0, 1), ("cov", 2), ("y", 0, 3), ("scores", 1, 2),
    ("scores", 0, 0), ("y", 0, 2), ("scores", 2, 1), ("scores", 2, 3), ("y", 3, 1), ("scores", 2, 2),
    ("scores", 3, 0), ("y", 3, 3), ("y", 3, 0), ("solve_in",), ("y", 3, 2), ("solve", 0),
    ("scores", 0, 1), ("norm", 1), ("scores", 0, 3), ("scores", 0, 2), ("solve", 1), ("norm", 2),
    ("solve", 2), ("scores", 3, 3), ("scores", 3, 1), ("scores", 3, 2), ("flush", 30), ("solve", 3), ("solve", 4),
    ("solve", 5), ("norm", 0), ("solve", 6), ("norm", 3), ("solve", 7), ("resid",),
)
DIRECT = {(0, 0), (0, 1), (0, 2), (0, 3), (1, 0), (1, 1), (1, 2), (1, 3), (2, 0), (2, 1), (2, 2), (2, 3), (3, 0), (3, 1), (3, 2), (3, 3)}


def kernel(
    dosage_hbm, scale_hbm, cov_hbm, prev_hbm, expr_hbm,
    resid_hbm, z_hbm,
    expr, geno, prev, dose, scale, cov_t, part, from_x, from_y, from_z, sums, full, system,
    ysq, from_ysq, y_factor, acc, xsq, from_acc, stat, resid,
    load_sem, send, recv, store_sem,
):
    s = lax.axis_index("samp")
    gene = lax.axis_index("gene")
    zh, y = gene // N, gene % N

    def peer(axis, step):
        if axis == "x":
            return {"samp": (s + step + N) % N}
        if axis == "y":
            return {"gene": zh * N + (y + step + N) % N}
        return {"gene": ((zh + step + N) % N) * N + y}

    peers = [peer(a, d) for a in "xyz" for d in (1, 2, 3)]
    barrier = pltpu.get_barrier_semaphore()
    for device in peers:
        pl.semaphore_signal(barrier, inc=1, device_id=device, device_id_type=pl.DeviceIdType.MESH)

    loads = [
        pltpu.make_async_copy(prev_hbm, prev, load_sem.at[0]),
        pltpu.make_async_copy(cov_hbm, cov_t, load_sem.at[1]),
        pltpu.make_async_copy(dosage_hbm, dose, load_sem.at[2]),
        pltpu.make_async_copy(scale_hbm, scale, load_sem.at[3]),
    ]
    for c in loads:
        c.start()
    panels = {}
    for ry in (0, 3, 1, 2):
        for rz in range(N):
            block = ((zh + rz) % N) * N + (y + ry) % N
            for half in (0, 1):
                start = pl.multiple_of(block * ROWS + half * PACK, 16)
                c = pltpu.make_async_copy(
                    expr_hbm.at[pl.ds(start, PACK)],
                    expr.at[ry, pl.ds(half * LINES + rz * PACK, PACK)],
                    load_sem.at[4 + (ry * N + rz) * 2 + half],
                )
                c.start()
                panels[ry, rz, half] = c

    loads[0].wait()
    left = lax.broadcasted_iota(jnp.int32, (PACK, 2 * CHUNK), 1) < CHUNK
    for c in range(CHUNKS):
        at = pl.ds(c // 2 * 2 * CHUNK, 2 * CHUNK)
        top, bottom = prev[:PACK, at].astype(F32), prev[PACK:, at].astype(F32)
        if c % 2 == 0:
            both = jnp.where(left, top, pltpu.roll(bottom, CHUNK, 1))
        else:
            both = jnp.where(left, pltpu.roll(top, CHUNK, 1), bottom)
        geno[c, 0, :PACK] = both.astype(BF16)
    ysq[...] = jnp.zeros((1, GENES), F32)
    pl.semaphore_wait(barrier, len(peers))

    sent = []
    ids = {}

    def push(name, src, dst, axis, step):
        t = len(sent)
        c = pltpu.make_async_remote_copy(
            src_ref=src, dst_ref=dst, send_sem=send.at[t], recv_sem=recv.at[t],
            device_id=peer(axis, step), device_id_type=pl.DeviceIdType.MESH,
        )
        c.start()
        sent.append(c)
        ids[name] = c

    landed = set()

    def arrive(*names):
        for name in names:
            if name not in landed:
                ids[name].wait_recv()
                landed.add(name)

    def rows(rz, lo=0, n=PACK):
        return pl.ds(rz * PACK + lo, n)

    def z_send(c):
        for step in (1, -1, 2):
            to = -step % N
            push(("z", c, to), geno.at[c, 0, rows(0)], geno.at[c, 0, rows(to)], "z", step)

    def y_go(c, rz):
        if rz:
            arrive(("z", c, rz))
        for step in (1, -1, 2) if (c, rz) in DIRECT else (1, -1):
            to = -step % N
            push(("y", c, to, rz), geno.at[c, 0, rows(rz)], geno.at[c, to, rows(rz)], "y", step)

    def y_pass(c, rz):
        arrive(("y", c, 3, rz))
        push(("y", c, 2, rz, 0), geno.at[c, 3, rows(rz, 0, CUT)], geno.at[c, 2, rows(rz, 0, CUT)], "y", 1)
        arrive(("y", c, 1, rz))
        push(("y", c, 2, rz, 1), geno.at[c, 1, rows(rz, CUT, PACK - CUT)], geno.at[c, 2, rows(rz, CUT, PACK - CUT)], "y", -1)

    def panel_arrive(c, ry):
        for rz in (0, 3, 1, 2):
            if ry == 0 and rz:
                arrive(("z", c, rz))
            elif ry in (1, 3) or (ry and (c, rz) in DIRECT):
                arrive(("y", c, ry, rz))
            elif ry:
                arrive(("y", c, 2, rz, 0), ("y", c, 2, rz, 1))

    def share(q):
        return pl.ds(pl.multiple_of(((s + q) % N) * SHARE, SHARE), SHARE)

    def cov_out():
        spot = lax.broadcasted_iota(jnp.int32, (COVS, AUG - SNP), 1)
        squares = jnp.zeros((COVS, AUG - SNP), F32)
        for c in range(CHUNKS):
            turned = geno[c, 0, :PACK].astype(F32).T
            column = jnp.sum(turned * turned, axis=1, keepdims=True)
            squares = jnp.where(spot == COVS + c, column[:CHUNK] + column[CHUNK:], squares)
        for c in loads[1:]:
            c.wait()
        part[:, :SNP] = jnp.dot(cov_t[...], dose[...].astype(F32), precision=HIGHEST, preferred_element_type=F32)
        part[:, SNP:] = squares
        part[:, SNP : SNP + COVS] = lax.dot_general(
            cov_t[...], cov_t[...], (((1,), (1,)), ((), ())), precision=HIGHEST, preferred_element_type=F32
        )
        for q in (1, 3, 2):
            push(("cx", q), part.at[share(q)], from_x.at[q - 1], "x", q)

    def cov(i):
        tag, landing, base = (("cx", from_x, part.at[share(0)]), ("cy", from_y, sums.at[0]), ("cz", from_z, sums.at[1]))[i]
        arrive(*[(tag, q) for q in (1, 3, 2)])
        sums[i] = base[...] + landing[0] + landing[1] + landing[2]
        for q in (1, 3, 2):
            if i == 0:
                push(("cy", q), sums.at[0], from_y.at[q - 1], "y", q)
            elif i == 1:
                push(("cz", q), sums.at[1], from_z.at[q - 1], "z", q)
            else:
                push(("cf", q), sums.at[2], full.at[N - q], "x", q)

    seen = set()

    def square(ry):
        total = jnp.zeros((8, GENES), F32)
        for half in (0, 1):
            for rz in range(N):
                if (ry, rz) not in seen:
                    panels[ry, rz, half].wait()

            def body(i, total):
                e = expr[ry, pl.ds(pl.multiple_of(half * LINES + i * 16, 16), 16), :].astype(F32)
                e = e * e
                return total + e[:8] + e[8:]

            total = lax.fori_loop(0, LINES // 16, body, total, unroll=6)
        seen.update((ry, rz) for rz in range(N))
        ysq[...] += jnp.sum(total, axis=0, keepdims=True)

    def ysq_out():
        for q in (1, 3, 2):
            push(("q", q), ysq, from_ysq.at[q - 1], "x", q)

    def piece(q):
        return pl.ds(pl.multiple_of(((s + q) % N) * OWN, OWN), OWN)

    begun = set()

    def scores(c, ry):
        first, last = c not in begun, ry == 2
        begun.add(c)
        for rz in range(N):
            for half in (0, 1):
                if (ry, rz) not in seen:
                    panels[ry, rz, half].wait()
            seen.add((ry, rz))
        panel_arrive(c, ry)
        turned = geno[c, ry].T
        lhs = jnp.concatenate([turned[:CHUNK], turned[CHUNK:]], axis=1)
        for j, (start, size) in enumerate(SPANS[c] if last else SPANS[3]):
            at = pl.ds(start, size)
            d = jnp.dot(lhs, expr[ry, :, at], preferred_element_type=F32)
            acc[c, :, at] = d if first else acc[c, :, at] + d
            if last:
                for q in (2, 1, 3):
                    push(("r", c, j, q), acc.at[c, piece(q), at], from_acc.at[c, q - 1, :, at], "x", q)

    stores = []

    def keep(src, dst):
        c = pltpu.make_async_copy(src, dst, store_sem.at[len(stores)])
        c.start()
        stores.append(c)

    def normalise(c):
        x_total = xsq[piece(0), :][:, COVS + c : COVS + c + 1]
        x_factor = jnp.sqrt(F32(SAMPLES)) / jnp.sqrt(x_total + 1e-6)
        out = pl.ds(pl.multiple_of(c * CHUNK + s * OWN, OWN), OWN)
        for j, (start, size) in enumerate(SPANS[c]):
            at = pl.ds(start, size)
            arrive(*[("r", c, j, q) for q in (1, 3, 2)])
            total = acc[c, piece(0), at] + from_acc[c, 0, :, at] + from_acc[c, 1, :, at] + from_acc[c, 2, :, at]
            stat[c, :, at] = (total * x_factor * y_factor[:, at]).astype(BF16)
            for q in (2, 1, 3):
                push(("s", c, j, q), stat.at[c, :, at], z_hbm.at[out, at], "x", q)
            keep(stat.at[c, :, at], z_hbm.at[out, at])

    def y_factors():
        arrive(*[("q", q) for q in (1, 3, 2)])
        y_total = ysq[...] + from_ysq[0] + from_ysq[1] + from_ysq[2]
        y_factor[...] = 1.0 / jnp.sqrt(y_total + 1e-6)

    def stat_done(c):
        for j in range(len(SPANS[c])):
            arrive(*[("s", c, j, q) for q in (1, 3, 2)])

    flushed = []

    def flush(recent=0):
        for c in sent[len(flushed) : len(sent) - recent]:
            c.wait_send()
            flushed.append(c)

    lane = lax.broadcasted_iota(jnp.int32, (COVS, 128), 1)
    line = lax.broadcasted_iota(jnp.int32, (COVS, AUG), 0)

    def solve_in():
        arrive(*[("cf", q) for q in (1, 3, 2)])
        system[share(0)] = sums[2]
        for q in (1, 2, 3):
            system[share(q)] = full[q]
        xsq[...] = system[:, SNP:]

    def eliminate(i):
        start, count = i * 8, 8

        def body(k, carry):
            a = system[...]
            row = system[pl.ds(k, 1), :]
            col = jnp.sum(jnp.where(lane == k, a[:, SNP:], 0.0), axis=1, keepdims=True)
            pivot = jnp.sum(jnp.where(lane[:1] == k, row[:, SNP:], 0.0), axis=1, keepdims=True)
            row = row / pivot
            system[...] = jnp.where(line == k, row, a - col * row)
            return carry

        lax.fori_loop(start, start + count, body, 0)

    def residual():
        fit = lax.dot_general(
            cov_t[...], system[:, :SNP], (((0,), (0,)), ((), ())), precision=HIGHEST, preferred_element_type=F32
        )
        resid[...] = ((dose[...].astype(F32) - fit) * scale[...]).astype(BF16)
        keep(resid, resid_hbm)

    steps = {
        "z": z_send, "y": y_go, "pass": y_pass, "cov_out": cov_out, "cov": cov, "square": square, "ysq": ysq_out,
        "y_factors": y_factors, "solve_in": solve_in, "solve": eliminate, "resid": residual, "scores": scores, "norm": normalise, "flush": flush,
    }
    for name, *at in ORDER:
        steps[name](*at)
    for c in range(CHUNKS):
        stat_done(c)
    flush()
    for c in stores:
        c.wait()


N_SENDS = 129
N_STORES = 10


def keep_all(resid_in, z_in, resid_out, z_out, resid_held, z_held, in_sem, out_sem):
    ways = [(resid_in, resid_held, resid_out)]
    for i in range(N):
        at = pl.ds(i * CHUNK, CHUNK)
        ways.append((z_in.at[at], z_held.at[at], z_out.at[at]))
    ins = [pltpu.make_async_copy(a, b, in_sem.at[i]) for i, (a, b, _) in enumerate(ways)]
    outs = [pltpu.make_async_copy(b, c, out_sem.at[i]) for i, (_, b, c) in enumerate(ways)]
    for copy in ins:
        copy.start()
    for first, then in zip(ins, outs):
        first.wait()
        then.start()
    for copy in outs:
        copy.wait()


def on_device(dosage, snp_scale, covariates, previous, expression):
    any_spec = pl.BlockSpec(memory_space=pl.ANY)
    resid, z = pl.pallas_call(
        kernel,
        out_shape=(
            jax.ShapeDtypeStruct((ROWS, SNP), BF16),
            jax.ShapeDtypeStruct((SNP, GENES), BF16),
        ),
        in_specs=[any_spec] * 5,
        out_specs=(any_spec, any_spec),
        scratch_shapes=[
            pltpu.VMEM((N, PANEL, GENES), BF16),
            pltpu.VMEM((CHUNKS, N, LINES, 2 * CHUNK), BF16),
            pltpu.VMEM((ROWS, SNP), BF16),
            pltpu.VMEM((ROWS, SNP), BF16),
            pltpu.VMEM((1, SNP), F32),
            pltpu.VMEM((COVS, ROWS), F32),
            pltpu.VMEM((COVS, AUG), F32),
            pltpu.VMEM((3, SHARE, AUG), F32),
            pltpu.VMEM((3, SHARE, AUG), F32),
            pltpu.VMEM((3, SHARE, AUG), F32),
            pltpu.VMEM((3, SHARE, AUG), F32),
            pltpu.VMEM((N, SHARE, AUG), F32),
            pltpu.VMEM((COVS, AUG), F32),
            pltpu.VMEM((1, GENES), F32),
            pltpu.VMEM((3, 1, GENES), F32),
            pltpu.VMEM((1, GENES), F32),
            pltpu.VMEM((CHUNKS, CHUNK, GENES), F32),
            pltpu.VMEM((COVS, AUG - SNP), F32),
            pltpu.VMEM((CHUNKS, 3, OWN, GENES), F32),
            pltpu.VMEM((CHUNKS, OWN, GENES), BF16),
            pltpu.VMEM((ROWS, SNP), BF16),
            pltpu.SemaphoreType.DMA((36,)),
            pltpu.SemaphoreType.DMA((N_SENDS,)),
            pltpu.SemaphoreType.DMA((N_SENDS,)),
            pltpu.SemaphoreType.DMA((N_STORES,)),
        ],
        compiler_params=pltpu.CompilerParams(
            collective_id=0, has_side_effects=True, vmem_limit_bytes=62 * 1024 * 1024
        ),
    )(dosage, snp_scale[None, :], covariates.T, previous, expression)
    return pl.pallas_call(
        keep_all,
        out_shape=(
            jax.ShapeDtypeStruct((ROWS, SNP), BF16),
            jax.ShapeDtypeStruct((SNP, GENES), BF16),
        ),
        in_specs=[any_spec] * 2,
        out_specs=(any_spec, any_spec),
        scratch_shapes=[
            pltpu.VMEM((ROWS, SNP), BF16),
            pltpu.VMEM((SNP, GENES), BF16),
            pltpu.SemaphoreType.DMA((N + 1,)),
            pltpu.SemaphoreType.DMA((N + 1,)),
        ],
        compiler_params=pltpu.CompilerParams(vmem_limit_bytes=62 * 1024 * 1024),
    )(resid, z)


def solution(mesh):
    placed = (
        P(("samp", "gene"), "snp"),
        P("snp"),
        P(("samp", "gene"), None),
        P(("samp", "gene"), "snp"),
        P("samp", "gene"),
    )
    return jax.shard_map(
        on_device,
        mesh=mesh,
        in_specs=placed,
        out_specs=(P(("samp", "gene"), "snp"), P("snp", "gene")),
        check_vma=False,
    )
```
